128 devices in a mesh: row: 16 (over x_hi, z, core), col: 8 (over x_lo, y).
Axes of the slice: x: 4 (x_hi: 2, x_lo: 2; x = x_hi * 2 + x_lo), y: 4, z: 4, core: 2. Of those that a mesh axis runs over, the one named last changes fastest.
Arguments:
- a_blocks: bfloat16 [16, 8, 32, 128, 128], P('row', 'col'), may hold values from -0.5 to 0.5
- b_blocks: bfloat16 [16, 8, 128, 128, 128], P('row', 'col'), may hold values from -1.5 to 1.5
- pairs: int32 [16, 8, 4, 3, 256], P('row', 'col'), may hold values from 0 to 127, as said below
Outputs:
- c_blocks: float32 [16, 8, 64, 128, 128], P('row', 'col')
The draws below stay inside these ranges and needn't reach their ends.
Inputs may be any that keep to these rules, and one draw needn't show every extreme that they name: `pairs`: rows 0 and 1 are slots of the left and right stacks; row 2 is a target block below 64, or 64 for a padded slot. Padded slots come after all live ones in each list. In every step some grid position has all 256 slots live and another has 64 live.
All inputs are finite; a program needn't handle non-finite values.
Results may differ from the reference program's by a relative error of at most 0.0003.
Values may be sent and summed in bfloat16 or wider, within the bound.
A program may use at most 128 MiB of HBM per device.

```python
import jax
import jax.numpy as jnp
from jax import lax

BS = 128
SA = 32
SB = 128
NP = 256
CBLK = 64
STEPS = 4
N_ROW = 16
N_COL = 8


def draw_pairs(key, part):
    subkeys = jax.random.split(jax.random.fold_in(key, 17), 5)
    grid_shape = (N_ROW, N_COL, STEPS, NP)
    left_slot = jax.random.randint(subkeys[0], grid_shape, 0, SA)
    right_slot = jax.random.randint(subkeys[1], grid_shape, 0, SB)
    target = jax.random.randint(subkeys[2], grid_shape, 0, CBLK)
    left_slot = left_slot.at[..., 0].set(SA - 1)
    right_slot = right_slot.at[..., 0].set(SB - 1)
    live_pairs = jax.random.randint(subkeys[3], (N_ROW * N_COL, STEPS), NP // 4, NP + 1)
    busiest = jax.random.randint(subkeys[4], (STEPS,), 0, N_ROW * N_COL)
    device = jnp.arange(N_ROW * N_COL)[:, None]
    live_pairs = jnp.where(device == busiest[None, :], NP, live_pairs)
    live_pairs = jnp.where(device == (busiest[None, :] + 1) % (N_ROW * N_COL), NP // 4, live_pairs)
    live_pairs = live_pairs.reshape(N_ROW, N_COL, STEPS, 1)
    target = jnp.where(jnp.arange(NP) < live_pairs, target, CBLK)
    return jnp.stack([left_slot, right_slot, target], axis=3).astype(jnp.int32)


def level_of(own_key, shape, cuts, least, largest):
    factor_of = 1.0
    for position, blocks in cuts:
        steps = jax.random.uniform(jax.random.fold_in(jax.random.fold_in(own_key, 6), position), (blocks,), jnp.float32, least / len(cuts), largest / len(cuts))
        factor_of = factor_of * jnp.repeat(jnp.exp(steps), shape[position] // blocks).reshape((-1,) + (1,) * (len(shape) - 1 - position))
    return factor_of


def noise(own_key, extent, deviation, reach, pieces=(), kind=jnp.bfloat16):
    entries = deviation * jax.random.normal(own_key, extent, jnp.float32)
    if pieces:
        entries = entries * level_of(own_key, extent, pieces, -0.22, 0.18)
    return jnp.clip(entries, -reach, reach).astype(kind)


def setup_inputs(seed: int = 0) -> dict:
    streams_of = jax.random.split(jax.random.key(seed), 4)
    return {
        "a_blocks": noise(streams_of[0], (N_ROW, N_COL, SA, BS, BS), BS ** -0.5, 0.5, ((0, 16), (1, 8))),
        "b_blocks": noise(streams_of[1], (N_ROW, N_COL, SB, BS, BS), 0.25, 1.5, ((0, 16), (1, 8))),
        "pairs": draw_pairs(jax.random.fold_in(streams_of[3], 71), 0),
    }


def reference(a_blocks, b_blocks, pairs):
    def one_device(device):
        grid_row = device // N_COL
        grid_col = device % N_COL
        running = jnp.zeros((CBLK + 1, BS, BS), jnp.float32)
        for section in range(STEPS):
            left_stack = a_blocks[grid_row, (grid_col - section) % N_COL]
            right_stack = b_blocks[(grid_row - section) % N_ROW, grid_col]
            pair_list = pairs[grid_row, grid_col, section]
            left = left_stack[pair_list[0]].astype(jnp.float32)
            right = right_stack[pair_list[1]].astype(jnp.float32)
            product = jnp.einsum("nij,njk->nik", left, right)
            running = running.at[pair_list[2]].add(product)
        return running[:CBLK]

    stacked = lax.map(one_device, jnp.arange(N_ROW * N_COL, dtype=jnp.int32))
    return stacked.reshape(N_ROW, N_COL, CBLK, BS, BS)
```

```python
import functools

import jax
import jax.numpy as jnp
from jax import lax
from jax.experimental import pallas as pl
from jax.experimental.pallas import tpu as pltpu
from jax.sharding import PartitionSpec as P

BS = 128
CBLK = 64
UNROLL = 16
PARTS = 2
HALF = CBLK // PARTS
ROWS = HALF * BS
AXES = ("row", "col")
VMEM = pl.BlockSpec(memory_space=pltpu.VMEM)
SMEM = pl.BlockSpec(memory_space=pltpu.SMEM)
LIMIT = pltpu.CompilerParams(vmem_limit_bytes=48 << 20)


def moved(value, rows, cols):
    n_row, n_col = lax.axis_size("row"), lax.axis_size("col")
    pairs = [
        (r * n_col + c, (r + rows) % n_row * n_col + (c + cols) % n_col)
        for r in range(n_row)
        for c in range(n_col)
    ]
    return lax.ppermute(value, AXES, pairs)


def live_slots(pairs_ref):
    slots = pairs_ref.shape[1]

    def halve(_, bounds):
        low, high = bounds
        middle = (low + high) // 2
        padded = pairs_ref[2, jnp.minimum(middle, slots - 1)] >= CBLK
        open_ = low < high
        return (
            jnp.where(open_ & ~padded, middle + 1, low),
            jnp.where(open_ & padded, middle, high),
        )

    low, _ = lax.fori_loop(0, slots.bit_length(), halve, (jnp.int32(0), jnp.int32(slots)))
    return low


def add_products(pairs_ref, a_ref, b_ref, acc):
    groups = (live_slots(pairs_ref) + UNROLL - 1) // UNROLL

    def group(g, carry):
        for u in range(UNROLL):
            n = g * UNROLL + u
            product = jnp.dot(
                a_ref[pairs_ref[0, n]], b_ref[pairs_ref[1, n]], preferred_element_type=jnp.float32
            )
            target = pairs_ref[2, n]
            acc[target] = acc[target] + product
        return carry

    lax.fori_loop(0, groups, group, 0)


def encode(value):
    top = jnp.max(jnp.abs(value), axis=0, keepdims=True)
    exponent = jnp.ceil(jnp.log2(jnp.maximum(top, 1e-30)) + 2e-4) - 15.0
    coded = jnp.round(value * jnp.exp2(-exponent)).astype(jnp.int32).astype(jnp.int16)
    return coded, exponent


def decode(coded, exponent):
    return coded.astype(jnp.int32).astype(jnp.float32) * jnp.exp2(exponent)


def encode_part(block_of, out_ref):
    def sixteen(g, carry):
        rows = []
        for u in range(16):
            c = g * 16 + u
            coded, exponent = block_of(c)
            out_ref[pl.ds(pl.multiple_of(c * BS, BS), BS), :] = coded
            rows.append(exponent)
        exponents = jnp.concatenate(rows, axis=0).astype(jnp.int32).astype(jnp.int16)
        out_ref[pl.ds(pl.multiple_of(ROWS + g * 16, 16), 16), :] = exponents
        return carry

    lax.fori_loop(0, HALF // 16, sixteen, 0)


def first_kernel(pairs_ref, a_ref, b_ref, *rest):
    out_refs, acc = rest[:PARTS], rest[PARTS]
    acc[...] = jnp.zeros_like(acc)
    add_products(pairs_ref, a_ref, b_ref, acc)
    for h in range(PARTS):
        encode_part(lambda c, h=h: encode(acc[h * HALF + c]), out_refs[h])


def product_kernel(pairs_ref, a_ref, b_ref, *rest):
    out_refs, acc = rest[:PARTS], rest[PARTS]
    acc[...] = jnp.zeros_like(acc)
    add_products(pairs_ref, a_ref, b_ref, acc)
    for h in range(PARTS):
        out_refs[h][...] = acc[pl.ds(h * HALF, HALF)]


def decoded_block(in_ref, exponents, c, u):
    return decode(in_ref[pl.ds(pl.multiple_of(c * BS, BS), BS), :], exponents[u : u + 1])


def middle_kernel(in_ref, sum_ref, out_ref):
    def sixteen(g, carry):
        exponents = in_ref[pl.ds(pl.multiple_of(ROWS + g * 16, 16), 16), :]
        exponents = exponents.astype(jnp.int32).astype(jnp.float32)
        rows = []
        for u in range(16):
            c = g * 16 + u
            coded, exponent = encode(sum_ref[c] + decoded_block(in_ref, exponents, c, u))
            out_ref[pl.ds(pl.multiple_of(c * BS, BS), BS), :] = coded
            rows.append(exponent)
        exponents = jnp.concatenate(rows, axis=0).astype(jnp.int32).astype(jnp.int16)
        out_ref[pl.ds(pl.multiple_of(ROWS + g * 16, 16), 16), :] = exponents
        return carry

    lax.fori_loop(0, HALF // 16, sixteen, 0)


def last_kernel(*refs):
    in_refs, sum_refs, out_ref = refs[:PARTS], refs[PARTS : 2 * PARTS], refs[2 * PARTS]
    for h in range(PARTS):

        def sixteen(g, carry, h=h):
            exponents = in_refs[h][pl.ds(pl.multiple_of(ROWS + g * 16, 16), 16), :]
            exponents = exponents.astype(jnp.int32).astype(jnp.float32)
            for u in range(16):
                c = g * 16 + u
                out_ref[h * HALF + c] = sum_refs[h][c] + decoded_block(in_refs[h], exponents, c, u)
            return carry

        lax.fori_loop(0, HALF // 16, sixteen, 0)


CODED = jax.ShapeDtypeStruct((ROWS + HALF, BS), jnp.int16)
SUM = jax.ShapeDtypeStruct((HALF, BS, BS), jnp.float32)
WORK = pl.CostEstimate(flops=2 * 256 * BS**3, bytes_accessed=16 << 20, transcendentals=0)
LIGHT = pl.CostEstimate(flops=1 << 22, bytes_accessed=8 << 20, transcendentals=0)


def multiply(kernel, out, pairs, a, b):
    return pl.pallas_call(
        kernel,
        out_shape=(out,) * PARTS,
        in_specs=[SMEM, VMEM, VMEM],
        out_specs=(VMEM,) * PARTS,
        scratch_shapes=[pltpu.VMEM((CBLK + 1, BS, BS), jnp.float32)],
        compiler_params=LIMIT,
        cost_estimate=WORK,
    )(pairs, a, b)


def middle(coded, own):
    return pl.pallas_call(
        middle_kernel,
        out_shape=CODED,
        in_specs=[VMEM, VMEM],
        out_specs=VMEM,
        compiler_params=LIMIT,
        cost_estimate=LIGHT,
    )(coded, own)


def last(coded, own):
    return pl.pallas_call(
        last_kernel,
        out_shape=jax.ShapeDtypeStruct((CBLK, BS, BS), jnp.float32),
        in_specs=[VMEM] * (2 * PARTS),
        out_specs=VMEM,
        compiler_params=LIMIT,
        cost_estimate=LIGHT,
    )(*coded, *own)


def on_device(a_blocks, b_blocks, pairs):
    a, b, lists = a_blocks[0, 0], b_blocks[0, 0], pairs[0, 0]
    steps = lists.shape[0]
    far = steps - 1
    running = None
    for s in range(far, -1, -1):
        left = moved(a, -s, s) if s else a
        listed = moved(lists[s], -s, 0) if s else lists[0]
        if s == far:
            running = multiply(first_kernel, CODED, listed, left, b)
        else:
            own = multiply(product_kernel, SUM, listed, left, b)
            arrived = [moved(part, 1, 0) for part in running]
            if s:
                running = [middle(x, y) for x, y in zip(arrived, own)]
            else:
                out = last(arrived, own)
    return out[None, None]


def solution(mesh):
    spec = P("row", "col", None, None, None)
    return jax.shard_map(
        on_device, mesh=mesh, in_specs=(spec,) * 3, out_specs=spec, check_vma=False
    )
```

```python
import jax
import jax.numpy as jnp
from jax import lax
from jax.experimental import pallas as pl
from jax.experimental.pallas import tpu as pltpu
from jax.sharding import PartitionSpec as P

BS = 128
SA = 32
SB = 128
NP = 256
CBLK = 64
STEPS = 4
UNROLL = 16
NC = 4
PER = CBLK // NC
CODED_ROWS = PER * BS + PER
NB = 4
BPER = SB // NB
NONE = NP
MESH = pl.DeviceIdType.MESH


def encode(value):
    top = jnp.max(jnp.abs(value), axis=0, keepdims=True)
    exponent = jnp.ceil(jnp.log2(jnp.maximum(top, 1e-30)) + 2e-4) - 15.0
    coded = jnp.round(value * jnp.exp2(-exponent)).astype(jnp.int32).astype(jnp.int16)
    return coded, exponent


def kernel(
    tables,
    a_hbm,
    b_hbm,
    out,
    a_one,
    a_two,
    a_even,
    a_odd,
    a_own,
    b_own,
    b_prev,
    b_mate,
    t_got,
    tab,
    tab_next,
    sums,
    acc,
    part,
    code_one,
    code_zero,
    code_in,
    a_recv,
    a_send,
    t_recv,
    t_send,
    mate_recv,
    mate_send,
    b_recv,
    b_send,
    c_recv,
    zero_send,
    one_send,
    local,
    smem_sem,
    out_sem,
):
    n_row, n_col = lax.axis_size("row"), lax.axis_size("col")
    row, col = lax.axis_index("row"), lax.axis_index("col")
    odd = lax.rem(row, 2)

    def at(rows, cols):
        return (lax.rem(row + rows + n_row, n_row), lax.rem(col + cols + n_col, n_col))

    def remote(src, dst, send, recv, to):
        return pltpu.make_async_remote_copy(
            src_ref=src, dst_ref=dst, send_sem=send, recv_sem=recv, device_id=to, device_id_type=MESH
        )

    def products(a, b, tab_ref, j):
        def group(g, carry):
            for u in range(UNROLL):
                n = g * UNROLL + u
                product = jnp.dot(
                    a[tab_ref[j, 0, n]], b[tab_ref[j, 1, n]], preferred_element_type=jnp.float32
                )
                sums[n] = sums[tab_ref[j, 2, n]] + product
            return carry

        lax.fori_loop(0, NP // UNROLL, group, 0)

    def collect(dst, tab_ref, j, add):
        def some(g, carry):
            for u in range(8):
                c = g * 8 + u
                value = sums[tab_ref[j, 3, c]]
                dst[c] = dst[c] + value if add else value
            return carry

        lax.fori_loop(0, CBLK // 8, some, 0)

    def encode_chunk(k, block_of, code):
        exponents = []
        for u in range(PER):
            coded, exponent = encode(block_of(k * PER + u))
            code[k, pl.ds(u * BS, BS), :] = coded
            exponents.append(exponent)
        rows = jnp.concatenate(exponents, axis=0).astype(jnp.int32).astype(jnp.int16)
        code[k, pl.ds(PER * BS, PER), :] = rows

    def a_copy(dst, slot, index, to):
        return remote(a_hbm, dst, a_send.at[slot], a_recv.at[index], to)

    def b_chunk(ref, k):
        return ref.at[pl.ds(k * BPER, BPER)]

    def bring(src, dst, k):
        copy = pltpu.make_async_copy(src, dst, local.at[k])
        copy.start()
        return copy

    def finish():
        def chunk(k, carry):
            remote(code_in.at[k], code_in.at[k], zero_send.at[k], c_recv.at[k], at(1, 0)).wait_recv()
            rows = code_in[k, pl.ds(PER * BS, PER), :].astype(jnp.int32).astype(jnp.float32)
            for u in range(PER):
                c = k * PER + u
                coded = code_in[k, pl.ds(u * BS, BS), :].astype(jnp.int32).astype(jnp.float32)
                acc[c] = acc[c] + coded * jnp.exp2(rows[u : u + 1])
            span = pl.ds(k * PER, PER)
            pltpu.make_async_copy(acc.at[span], out.at[span], out_sem.at[k]).start()
            return carry

        lax.fori_loop(0, NC, chunk, 0)

        def drained(k, carry):
            span = pl.ds(k * PER, PER)
            pltpu.make_async_copy(acc.at[span], out.at[span], out_sem.at[k]).wait()
            return carry

        lax.fori_loop(0, NC, drained, 0)

    barrier = pltpu.get_barrier_semaphore()

    def greet(sources, targets):
        for to in sources:
            pl.semaphore_signal(barrier, inc=1, device_id=at(*to), device_id_type=MESH)
        pl.semaphore_wait(barrier, targets)

    @pl.when(odd == 0)
    def _():
        greet([(0, -1), (2, -2), (2, -3), (3, -3), (2, 0), (3, 0), (-1, 0), (-2, 0)], 7)

    @pl.when(odd == 1)
    def _():
        greet([(0, -1), (0, -2), (-1, 0), (-3, 0)], 5)

    @pl.when(odd == 0)
    def _():
        left = a_copy(a_one, 0, 0, at(0, 1))
        left.start()
        listed = remote(
            tables.at[pl.ds(2, 2)], t_got.at[pl.ds(0, 2)], t_send.at[0], t_recv.at[0], at(-2, 0)
        )
        listed.start()
        mate = remote(b_hbm, b_mate, mate_send.at[0], mate_recv.at[0], at(1, 0))
        mate.start()
        own_tab = bring(tables, tab, 0)
        own_a = bring(a_hbm, a_own, 1)
        own_b = bring(b_hbm, b_own, 2)
        sums[NONE] = jnp.zeros((BS, BS), jnp.float32)
        own_tab.wait()
        own_a.wait()
        own_b.wait()
        products(a_own, b_own, tab, 0)
        collect(acc, tab, 0, False)
        listed.wait_recv()
        remote(
            tables.at[pl.ds(3, 1)], t_got.at[pl.ds(2, 1)], t_send.at[0], t_recv.at[1], at(1, 0)
        ).wait_recv()
        got = pltpu.make_async_copy(t_got, tab_next, smem_sem.at[0])
        got.start()
        left.wait_send()
        far = a_copy(a_even, 1, 2, at(-2, 3))
        far.start()
        got.wait()
        a_copy(a_odd, 2, 3, at(1, 0)).wait_recv()
        products(a_odd, b_own, tab_next, 2)

        def one(k, carry):
            encode_chunk(k, lambda c: sums[tab_next[2, 3, c]], code_one)
            return carry

        lax.fori_loop(0, NC, one, 0)
        far.wait_send()
        two = a_copy(a_two, 2, 1, at(-2, 2))
        two.start()
        two.wait_recv()
        products(a_two, b_own, tab_next, 0)
        collect(part, tab_next, 0, False)

        def pass_on(k, carry):
            copy = remote(
                b_chunk(b_prev, k), b_chunk(b_prev, k), b_send.at[k], b_recv.at[k], at(1, 0)
            )
            copy.wait_recv()
            copy.start()
            return carry

        lax.fori_loop(0, NB, pass_on, 0)

        def send_one(k, carry):
            remote(code_one.at[k], code_in.at[k], one_send.at[k], c_recv.at[k], at(3, 0)).start()
            return carry

        lax.fori_loop(0, NC, send_one, 0)
        far.wait_recv()
        products(a_even, b_prev, tab_next, 1)

        def zero(k, carry):
            encode_chunk(k, lambda c: part[c] + sums[tab_next[1, 3, c]], code_zero)
            remote(code_zero.at[k], code_in.at[k], zero_send.at[k], c_recv.at[k], at(2, 0)).start()
            return carry

        lax.fori_loop(0, NC, zero, 0)
        left.wait_recv()
        products(a_one, b_prev, tab, 1)
        collect(acc, tab, 1, True)
        two.wait_send()
        listed.wait_send()
        mate.wait_send()
        finish()

        def drained(k, carry):
            remote(
                b_chunk(b_prev, k), b_chunk(b_prev, k), b_send.at[k], b_recv.at[k], at(1, 0)
            ).wait_send()
            return carry

        lax.fori_loop(0, NB, drained, 0)

        def gone(k, carry):
            remote(code_one.at[k], code_in.at[k], one_send.at[k], c_recv.at[k], at(3, 0)).wait_send()
            remote(code_zero.at[k], code_in.at[k], zero_send.at[k], c_recv.at[k], at(2, 0)).wait_send()
            return carry

        lax.fori_loop(0, NC, gone, 0)

    @pl.when(odd == 1)
    def _():
        def give(k, carry):
            remote(
                b_chunk(b_hbm, k), b_chunk(b_prev, k), b_send.at[k], b_recv.at[k], at(1, 0)
            ).start()
            return carry

        lax.fori_loop(0, NB, give, 0)
        far = a_copy(a_odd, 0, 3, at(-3, 3))
        far.start()
        listed = remote(
            tables.at[pl.ds(3, 1)], t_got.at[pl.ds(2, 1)], t_send.at[0], t_recv.at[1], at(-3, 0)
        )
        listed.start()
        own_tab = bring(tables, tab, 0)
        own_a = bring(a_hbm, a_own, 1)
        own_b = bring(b_hbm, b_own, 2)
        sums[NONE] = jnp.zeros((BS, BS), jnp.float32)
        own_tab.wait()
        own_a.wait()
        own_b.wait()
        products(a_own, b_own, tab, 0)
        collect(acc, tab, 0, False)
        far.wait_send()
        left = a_copy(a_one, 1, 0, at(0, 1))
        left.start()
        remote(b_hbm, b_mate, mate_send.at[0], mate_recv.at[0], at(-1, 0)).wait_recv()
        left.wait_recv()
        products(a_one, b_mate, tab, 1)
        collect(acc, tab, 1, True)
        left.wait_send()
        two = a_copy(a_two, 2, 1, at(0, 2))
        two.start()
        two.wait_recv()

        def arrived(k, carry):
            remote(
                b_chunk(b_prev, k), b_chunk(b_prev, k), b_send.at[k], b_recv.at[k], at(1, 0)
            ).wait_recv()
            return carry

        lax.fori_loop(0, NB, arrived, 0)
        products(a_two, b_prev, tab, 2)
        collect(acc, tab, 2, True)
        two.wait_send()
        listed.wait_send()

        def drained(k, carry):
            remote(
                b_chunk(b_hbm, k), b_chunk(b_prev, k), b_send.at[k], b_recv.at[k], at(1, 0)
            ).wait_send()
            return carry

        lax.fori_loop(0, NB, drained, 0)
        finish()


def grid_product(tables, a, b):
    anywhere = pl.BlockSpec(memory_space=pl.ANY)
    left = pltpu.VMEM((SA, BS, BS), jnp.bfloat16)
    right = pltpu.VMEM((SB, BS, BS), jnp.bfloat16)
    code = pltpu.VMEM((NC, CODED_ROWS, BS), jnp.int16)
    dma = pltpu.SemaphoreType.DMA
    return pl.pallas_call(
        kernel,
        out_shape=jax.ShapeDtypeStruct((CBLK, BS, BS), jnp.float32),
        in_specs=[anywhere] * 3,
        out_specs=anywhere,
        scratch_shapes=[left] * 5
        + [right] * 3
        + [
            pltpu.VMEM((3, 4, NP), jnp.int32),
            pltpu.SMEM((STEPS, 4, NP), jnp.int32),
            pltpu.SMEM((3, 4, NP), jnp.int32),
            pltpu.VMEM((NP + 1, BS, BS), jnp.float32),
            pltpu.VMEM((CBLK, BS, BS), jnp.float32),
            pltpu.VMEM((CBLK, BS, BS), jnp.float32),
        ]
        + [code] * 3
        + [
            dma((4,)),
            dma((3,)),
            dma((2,)),
            dma((1,)),
            dma((1,)),
            dma((1,)),
            dma((NB,)),
            dma((NB,)),
            dma((NC,)),
            dma((NC,)),
            dma((NC,)),
            dma((3,)),
            dma((1,)),
            dma((NC,)),
        ],
        compiler_params=pltpu.CompilerParams(
            collective_id=0, has_side_effects=True, vmem_limit_bytes=58 << 20
        ),
        cost_estimate=pl.CostEstimate(
            flops=2 * STEPS * NP * BS**3, bytes_accessed=32 << 20, transcendentals=0
        ),
    )(tables, a, b)


def listed(pairs):
    target = pairs[:, 2, :]
    slot = jnp.arange(NP, dtype=jnp.int32)
    same = (target[:, :, None] == target[:, None, :]) & (slot[:, None] < slot[None, :])
    before = jnp.max(jnp.where(same, slot[:, None], -1), axis=1)
    hit = target[:, :, None] == slot[None, None, :]
    final = jnp.max(jnp.where(hit, slot[:, None], -1), axis=1)
    found = jnp.stack([before, final], axis=1)
    found = jnp.where(found < 0, NONE, found)
    return jnp.concatenate([pairs[:, :2, :], found], axis=1)


def on_device(a_blocks, b_blocks, pairs):
    return grid_product(listed(pairs[0, 0]), a_blocks[0, 0], b_blocks[0, 0])[None, None]


def solution(mesh):
    spec = P("row", "col", None, None, None)
    return jax.shard_map(
        on_device, mesh=mesh, in_specs=(spec,) * 3, out_specs=spec, check_vma=False
    )
```

```python
import jax
import jax.numpy as jnp
from jax import lax
from jax.experimental import pallas as pl
from jax.experimental.pallas import tpu as pltpu
from jax.sharding import PartitionSpec as P

BS = 128
SA = 32
SB = 128
NP = 256
CBLK = 64
STEPS = 4
UNROLL = 16
NC = 4
PER = CBLK // NC
CODED_ROWS = PER * BS + PER
NB = 4
BPER = SB // NB
RELAYED = (3,)
DIRECT = tuple(k for k in range(NB) if k not in RELAYED)
NONE = NP
MESH = pl.DeviceIdType.MESH


def encode(value):
    top = jnp.max(jnp.abs(value), axis=0, keepdims=True)
    exponent = jnp.ceil(jnp.log2(jnp.maximum(top, 1e-30)) + 2e-4) - 15.0
    coded = jnp.round(value * jnp.exp2(-exponent)).astype(jnp.int32).astype(jnp.int16)
    return coded, exponent


def kernel(
    tables,
    a_hbm,
    b_hbm,
    out,
    a_one,
    a_two,
    a_even,
    a_odd,
    a_own,
    a_flip,
    b_own,
    b_prev,
    b_mate,
    t_got,
    tab,
    tab_next,
    sums,
    acc,
    part,
    code_one,
    code_zero,
    code_in,
    a_recv,
    a_send,
    t_recv,
    t_send,
    mate_recv,
    mate_send,
    b_recv,
    b_send,
    hub_recv,
    hub_send,
    c_recv,
    zero_send,
    one_send,
    local,
    smem_sem,
    out_sem,
):
    n_row, n_col = lax.axis_size("row"), lax.axis_size("col")
    row, col = lax.axis_index("row"), lax.axis_index("col")
    odd = lax.rem(row, 2)

    def at(rows, cols):
        return (lax.rem(row + rows + n_row, n_row), lax.rem(col + cols + n_col, n_col))

    def remote(src, dst, send, recv, to):
        return pltpu.make_async_remote_copy(
            src_ref=src, dst_ref=dst, send_sem=send, recv_sem=recv, device_id=to, device_id_type=MESH
        )

    def products(a, b, tab_ref, j):
        def group(g, carry):
            for u in range(UNROLL):
                n = g * UNROLL + u
                product = jnp.dot(
                    a[tab_ref[j, 0, n]], b[tab_ref[j, 1, n]], preferred_element_type=jnp.float32
                )
                sums[n] = sums[tab_ref[j, 2, n]] + product
            return carry

        lax.fori_loop(0, NP // UNROLL, group, 0)

    def collect(dst, tab_ref, j, add):
        def some(g, carry):
            for u in range(8):
                c = g * 8 + u
                value = sums[tab_ref[j, 3, c]]
                dst[c] = dst[c] + value if add else value
            return carry

        lax.fori_loop(0, CBLK // 8, some, 0)

    def encode_chunk(k, block_of, code):
        exponents = []
        for u in range(PER):
            coded, exponent = encode(block_of(k * PER + u))
            code[k, pl.ds(u * BS, BS), :] = coded
            exponents.append(exponent)
        rows = jnp.concatenate(exponents, axis=0).astype(jnp.int32).astype(jnp.int16)
        code[k, pl.ds(PER * BS, PER), :] = rows

    lane = lax.rem(col, n_col // 2)
    plane = col - lane

    def along(rows, steps):
        half = n_col // 2
        return (lax.rem(row + rows + n_row, n_row), plane + lax.rem(lane + steps + half, half))

    def a_copy(dst, slot, index, to, src=None):
        return remote(a_hbm if src is None else src, dst, a_send.at[slot], a_recv.at[index], to)

    def a_start(dst, slot, index, to, steps):
        @pl.when(lane + steps < n_col // 2)
        def _():
            a_copy(dst, slot, index, to).start()

        @pl.when(lane + steps >= n_col // 2)
        def _():
            a_copy(dst, slot, index, to, a_flip).start()

    def b_chunk(ref, k):
        return ref.at[pl.ds(k * BPER, BPER)]

    def bring(src, dst, k):
        copy = pltpu.make_async_copy(src, dst, local.at[k])
        copy.start()
        return copy

    def finish():
        def chunk(k, carry):
            remote(code_in.at[k], code_in.at[k], zero_send.at[k], c_recv.at[k], at(1, 0)).wait_recv()
            rows = code_in[k, pl.ds(PER * BS, PER), :].astype(jnp.int32).astype(jnp.float32)
            for u in range(PER):
                c = k * PER + u
                coded = code_in[k, pl.ds(u * BS, BS), :].astype(jnp.int32).astype(jnp.float32)
                acc[c] = acc[c] + coded * jnp.exp2(rows[u : u + 1])
            span = pl.ds(k * PER, PER)
            pltpu.make_async_copy(acc.at[span], out.at[span], out_sem.at[k]).start()
            return carry

        lax.fori_loop(0, NC, chunk, 0)

        def drained(k, carry):
            span = pl.ds(k * PER, PER)
            pltpu.make_async_copy(acc.at[span], out.at[span], out_sem.at[k]).wait()
            return carry

        lax.fori_loop(0, NC, drained, 0)

    barrier = pltpu.get_barrier_semaphore()
    place = lax.rem(row, n_row // 2)
    at_start = place == 0
    hub = place == 1
    seam = place == n_row // 2 - 1
    across = n_row // 2

    def hail(to):
        pl.semaphore_signal(barrier, inc=1, device_id=to, device_id_type=MESH)

    @pl.when(odd == 0)
    def _():
        for rows, steps in ((0, -1), (2, -2), (2, -3), (3, -3)):
            hail(along(rows, steps))
        for rows, cols in ((0, n_col // 2), (2, 0), (3, 0), (-1, 0), (-2, 0)):
            hail(at(rows, cols))

        @pl.when(at_start)
        def _():
            hail(at(across + 1, 0))

        pl.semaphore_wait(barrier, 8)

    @pl.when(odd == 1)
    def _():
        for rows, steps in ((0, -1), (0, -2)):
            hail(along(rows, steps))
        for rows, cols in ((0, n_col // 2), (-1, 0), (-3, 0)):
            hail(at(rows, cols))

        @pl.when(hub)
        def _():
            hail(at(across - 2, 0))

        pl.semaphore_wait(barrier, 6 + jnp.where(hub | seam, 1, 0))

    flip = a_copy(a_flip, 3, 4, at(0, n_col // 2))
    flip.start()

    @pl.when(odd == 0)
    def _():
        @pl.when(lane + 1 < n_col // 2)
        def _():
            a_copy(a_one, 0, 0, along(0, 1)).start()

        listed = remote(
            tables.at[pl.ds(2, 2)], t_got.at[pl.ds(0, 2)], t_send.at[0], t_recv.at[0], at(-2, 0)
        )
        listed.start()
        mate = remote(b_hbm, b_mate, mate_send.at[0], mate_recv.at[0], at(1, 0))
        mate.start()
        own_tab = bring(tables, tab, 0)
        own_a = bring(a_hbm, a_own, 1)
        own_b = bring(b_hbm, b_own, 2)
        sums[NONE] = jnp.zeros((BS, BS), jnp.float32)
        own_tab.wait()
        own_a.wait()
        own_b.wait()
        products(a_own, b_own, tab, 0)
        collect(acc, tab, 0, False)
        flip.wait_recv()
        left = a_copy(a_one, 0, 0, along(0, 1))
        far = a_copy(a_even, 2, 2, along(-2, 3))
        two = a_copy(a_two, 1, 1, along(-2, 2))
        a_start(a_even, 2, 2, along(-2, 3), 3)

        @pl.when(lane + 1 >= n_col // 2)
        def _():
            a_copy(a_one, 0, 0, along(0, 1), a_flip).start()

        listed.wait_recv()
        remote(
            tables.at[pl.ds(3, 1)], t_got.at[pl.ds(2, 1)], t_send.at[0], t_recv.at[1], at(1, 0)
        ).wait_recv()
        got = pltpu.make_async_copy(t_got, tab_next, smem_sem.at[0])
        got.start()
        got.wait()
        far.wait_send()
        a_start(a_two, 1, 1, along(-2, 2), 2)
        a_copy(a_odd, 2, 3, at(1, 0)).wait_recv()
        products(a_odd, b_own, tab_next, 2)

        def one(k, carry):
            encode_chunk(k, lambda c: sums[tab_next[2, 3, c]], code_one)
            return carry

        lax.fori_loop(0, NC, one, 0)

        def send_one(k, carry):
            remote(code_one.at[k], code_in.at[k], one_send.at[k], c_recv.at[k], at(3, 0)).start()
            return carry

        @pl.when(at_start)
        def _():
            lax.fori_loop(0, NC, send_one, 0)

        def pass_on(k, carry):
            copy = remote(
                b_chunk(b_prev, k), b_chunk(b_prev, k), b_send.at[k], b_recv.at[k], at(1, 0)
            )
            copy.wait_recv()
            copy.start()
            return carry

        lax.fori_loop(0, NB, pass_on, 0)

        @pl.when(jnp.logical_not(at_start))
        def _():
            lax.fori_loop(0, NC, send_one, 0)

        far.wait_recv()
        products(a_even, b_prev, tab_next, 1)
        collect(part, tab_next, 1, False)
        two.wait_recv()
        products(a_two, b_own, tab_next, 0)

        def zero(k, carry):
            encode_chunk(k, lambda c: part[c] + sums[tab_next[0, 3, c]], code_zero)
            remote(code_zero.at[k], code_in.at[k], zero_send.at[k], c_recv.at[k], at(2, 0)).start()
            return carry

        lax.fori_loop(0, NC, zero, 0)
        left.wait_recv()
        products(a_one, b_prev, tab, 1)
        collect(acc, tab, 1, True)
        left.wait_send()
        two.wait_send()
        flip.wait_send()
        listed.wait_send()
        mate.wait_send()

        def drained(k, carry):
            remote(
                b_chunk(b_prev, k), b_chunk(b_prev, k), b_send.at[k], b_recv.at[k], at(1, 0)
            ).wait_send()
            return carry

        lax.fori_loop(0, NB, drained, 0)
        finish()

        def gone(k, carry):
            remote(code_one.at[k], code_in.at[k], one_send.at[k], c_recv.at[k], at(3, 0)).wait_send()
            remote(code_zero.at[k], code_in.at[k], zero_send.at[k], c_recv.at[k], at(2, 0)).wait_send()
            return carry

        lax.fori_loop(0, NC, gone, 0)

    @pl.when(odd == 1)
    def _():
        def b_copy(k):
            return remote(
                b_chunk(b_hbm, k), b_chunk(b_prev, k), b_send.at[k], b_recv.at[k], at(1, 0)
            )

        def to_hub(k):
            return remote(
                b_chunk(b_hbm, k),
                (a_even, a_odd)[k - 2],
                b_send.at[k],
                hub_recv.at[k - 2],
                at(2 - across, 0),
            )

        def from_hub(k):
            return remote(
                (a_even, a_odd)[k - 2],
                b_chunk(b_prev, k),
                hub_send.at[k - 2],
                b_recv.at[k],
                at(across - 1, 0),
            )

        @pl.when(seam)
        def _():
            for k in RELAYED:
                to_hub(k).start()

        @pl.when(jnp.logical_not(seam))
        def _():
            for k in range(NB):
                b_copy(k).start()

        listed = remote(
            tables.at[pl.ds(3, 1)], t_got.at[pl.ds(2, 1)], t_send.at[0], t_recv.at[1], at(-3, 0)
        )
        listed.start()
        own_tab = bring(tables, tab, 0)
        own_a = bring(a_hbm, a_own, 1)
        own_b = bring(b_hbm, b_own, 2)

        @pl.when(lane + 1 < n_col // 2)
        def _():
            a_copy(a_one, 0, 0, along(0, 1)).start()

        sums[NONE] = jnp.zeros((BS, BS), jnp.float32)
        own_tab.wait()
        own_a.wait()
        own_b.wait()
        products(a_own, b_own, tab, 0)
        collect(acc, tab, 0, False)
        flip.wait_recv()
        left = a_copy(a_one, 0, 0, along(0, 1))
        far = a_copy(a_odd, 2, 3, along(-3, 3))
        two = a_copy(a_two, 1, 1, along(0, 2))
        a_start(a_odd, 2, 3, along(-3, 3), 3)

        @pl.when(lane + 1 >= n_col // 2)
        def _():
            a_copy(a_one, 0, 0, along(0, 1), a_flip).start()

        @pl.when(seam)
        def _():
            for k in DIRECT:
                b_copy(k).start()

        remote(b_hbm, b_mate, mate_send.at[0], mate_recv.at[0], at(-1, 0)).wait_recv()
        left.wait_recv()
        products(a_one, b_mate, tab, 1)
        collect(acc, tab, 1, True)
        far.wait_send()
        a_start(a_two, 1, 1, along(0, 2), 2)

        @pl.when(hub)
        def _():
            for k in RELAYED:
                to_hub(k).wait_recv()
                from_hub(k).start()

        two.wait_recv()
        for k in range(NB):
            b_copy(k).wait_recv()
        products(a_two, b_prev, tab, 2)
        collect(acc, tab, 2, True)
        left.wait_send()
        two.wait_send()
        flip.wait_send()
        listed.wait_send()
        for k in range(NB):
            b_copy(k).wait_send()

        @pl.when(hub)
        def _():
            for k in RELAYED:
                from_hub(k).wait_send()

        finish()


def grid_product(tables, a, b):
    anywhere = pl.BlockSpec(memory_space=pl.ANY)
    left = pltpu.VMEM((SA, BS, BS), jnp.bfloat16)
    right = pltpu.VMEM((SB, BS, BS), jnp.bfloat16)
    code = pltpu.VMEM((NC, CODED_ROWS, BS), jnp.int16)
    dma = pltpu.SemaphoreType.DMA
    return pl.pallas_call(
        kernel,
        out_shape=jax.ShapeDtypeStruct((CBLK, BS, BS), jnp.float32),
        in_specs=[anywhere] * 3,
        out_specs=anywhere,
        scratch_shapes=[left] * 6
        + [right] * 3
        + [
            pltpu.VMEM((3, 4, NP), jnp.int32),
            pltpu.SMEM((STEPS, 4, NP), jnp.int32),
            pltpu.SMEM((3, 4, NP), jnp.int32),
            pltpu.VMEM((NP + 1, BS, BS), jnp.float32),
            pltpu.VMEM((CBLK, BS, BS), jnp.float32),
            pltpu.VMEM((CBLK, BS, BS), jnp.float32),
        ]
        + [code] * 3
        + [
            dma((5,)),
            dma((4,)),
            dma((2,)),
            dma((1,)),
            dma((1,)),
            dma((1,)),
            dma((NB,)),
            dma((NB,)),
            dma((2,)),
            dma((2,)),
            dma((NC,)),
            dma((NC,)),
            dma((NC,)),
            dma((3,)),
            dma((1,)),
            dma((NC,)),
        ],
        compiler_params=pltpu.CompilerParams(
            collective_id=0, has_side_effects=True, vmem_limit_bytes=58 << 20
        ),
        cost_estimate=pl.CostEstimate(
            flops=2 * STEPS * NP * BS**3, bytes_accessed=32 << 20, transcendentals=0
        ),
    )(tables, a, b)


def listed(pairs):
    target = pairs[:, 2, :]
    slot = jnp.arange(NP, dtype=jnp.int32)
    same = (target[:, :, None] == target[:, None, :]) & (slot[:, None] < slot[None, :])
    before = jnp.max(jnp.where(same, slot[:, None], -1), axis=1)
    hit = target[:, :, None] == slot[None, None, :]
    final = jnp.max(jnp.where(hit, slot[:, None], -1), axis=1)
    found = jnp.stack([before, final], axis=1)
    found = jnp.where(found < 0, NONE, found)
    return jnp.concatenate([pairs[:, :2, :], found], axis=1)


def on_device(a_blocks, b_blocks, pairs):
    return grid_product(listed(pairs[0, 0]), a_blocks[0, 0], b_blocks[0, 0])[None, None]


def solution(mesh):
    spec = P("row", "col", None, None, None)
    return jax.shard_map(
        on_device, mesh=mesh, in_specs=(spec,) * 3, out_specs=spec, check_vma=False
    )
```

```python
import jax
import jax.numpy as jnp
from jax import lax
from jax.experimental import pallas as pl
from jax.experimental.pallas import tpu as pltpu
from jax.sharding import PartitionSpec as P

BS = 128
SA = 32
SB = 128
NP = 256
CBLK = 64
STEPS = 4
UNROLL = 16
NC = 4
PER = CBLK // NC
CODED_ROWS = PER * BS + PER
NB = 4
BPER = SB // NB
RELAYED = (3,)
DIRECT = tuple(k for k in range(NB) if k not in RELAYED)
NONE = NP
MESH = pl.DeviceIdType.MESH


def encode(value):
    top = jnp.max(jnp.abs(value), axis=0, keepdims=True)
    exponent = jnp.ceil(jnp.log2(jnp.maximum(top, 1e-30)) + 2e-4) - 15.0
    coded = jnp.round(value * jnp.exp2(-exponent)).astype(jnp.int32).astype(jnp.int16)
    return coded, exponent


def kernel(
    tables,
    a_hbm,
    b_hbm,
    out,
    a_one,
    a_two,
    a_even,
    a_odd,
    a_own,
    a_flip,
    b_own,
    b_prev,
    b_mate,
    t_got,
    tab,
    tab_next,
    sums,
    acc,
    part,
    code_one,
    code_zero,
    code_in,
    a_recv,
    a_send,
    t_recv,
    t_send,
    mate_recv,
    mate_send,
    b_recv,
    b_send,
    hub_recv,
    hub_send,
    c_recv,
    zero_send,
    one_send,
    local,
    smem_sem,
    out_sem,
):
    n_row, n_col = lax.axis_size("row"), lax.axis_size("col")
    row, col = lax.axis_index("row"), lax.axis_index("col")
    odd = lax.rem(row, 2)

    def at(rows, cols):
        return (lax.rem(row + rows + n_row, n_row), lax.rem(col + cols + n_col, n_col))

    def remote(src, dst, send, recv, to):
        return pltpu.make_async_remote_copy(
            src_ref=src, dst_ref=dst, send_sem=send, recv_sem=recv, device_id=to, device_id_type=MESH
        )

    def products(a, b, tab_ref, j):
        def group(g, carry):
            for u in range(UNROLL):
                n = g * UNROLL + u
                product = jnp.dot(
                    a[tab_ref[j, 0, n]], b[tab_ref[j, 1, n]], preferred_element_type=jnp.float32
                )
                sums[n] = sums[tab_ref[j, 2, n]] + product
            return carry

        lax.fori_loop(0, NP // UNROLL, group, 0)

    def collect(dst, tab_ref, j, add):
        def some(g, carry):
            for u in range(8):
                c = g * 8 + u
                value = sums[tab_ref[j, 3, c]]
                dst[c] = dst[c] + value if add else value
            return carry

        lax.fori_loop(0, CBLK // 8, some, 0)

    def encode_chunk(k, block_of, code):
        exponents = []
        for u in range(PER):
            coded, exponent = encode(block_of(k * PER + u))
            code[k, pl.ds(u * BS, BS), :] = coded
            exponents.append(exponent)
        rows = jnp.concatenate(exponents, axis=0).astype(jnp.int32).astype(jnp.int16)
        code[k, pl.ds(PER * BS, PER), :] = rows

    lane = lax.rem(col, n_col // 2)
    plane = col - lane

    def along(rows, steps):
        half = n_col // 2
        return (lax.rem(row + rows + n_row, n_row), plane + lax.rem(lane + steps + half, half))

    def a_copy(dst, slot, index, to, src=None):
        return remote(a_hbm if src is None else src, dst, a_send.at[slot], a_recv.at[index], to)

    def a_start(dst, slot, index, to, steps):
        @pl.when(lane + steps < n_col // 2)
        def _():
            a_copy(dst, slot, index, to).start()

        @pl.when(lane + steps >= n_col // 2)
        def _():
            a_copy(dst, slot, index, to, a_flip).start()

    def b_chunk(ref, k):
        return ref.at[pl.ds(k * BPER, BPER)]

    def bring(src, dst, k):
        copy = pltpu.make_async_copy(src, dst, local.at[k])
        copy.start()
        return copy

    def absorb(k):
        remote(code_in.at[k], code_in.at[k], zero_send.at[k], c_recv.at[k], at(1, 0)).wait_recv()
        rows = code_in[k, pl.ds(PER * BS, PER), :].astype(jnp.int32).astype(jnp.float32)
        for u in range(PER):
            c = k * PER + u
            coded = code_in[k, pl.ds(u * BS, BS), :].astype(jnp.int32).astype(jnp.float32)
            acc[c] = acc[c] + coded * jnp.exp2(rows[u : u + 1])

    def finish():
        def chunk(k, carry):
            absorb(k)
            span = pl.ds(k * PER, PER)
            pltpu.make_async_copy(acc.at[span], out.at[span], out_sem.at[k]).start()
            return carry

        lax.fori_loop(0, NC, chunk, 0)

        def drained(k, carry):
            span = pl.ds(k * PER, PER)
            pltpu.make_async_copy(acc.at[span], out.at[span], out_sem.at[k]).wait()
            return carry

        lax.fori_loop(0, NC, drained, 0)

    barrier = pltpu.get_barrier_semaphore()
    place = lax.rem(row, n_row // 2)
    at_start = place == 0
    hub = place == 1
    seam = place == n_row // 2 - 1
    across = n_row // 2

    def hail(to):
        pl.semaphore_signal(barrier, inc=1, device_id=to, device_id_type=MESH)

    @pl.when(odd == 0)
    def _():
        for rows, steps in ((0, -1), (2, -2), (2, -3), (3, -3)):
            hail(along(rows, steps))
        for rows, cols in ((0, n_col // 2), (2, 0), (3, 0), (-1, 0), (-2, 0)):
            hail(at(rows, cols))

        @pl.when(at_start)
        def _():
            hail(at(across + 1, 0))

        pl.semaphore_wait(barrier, 8)

    @pl.when(odd == 1)
    def _():
        for rows, steps in ((0, -1), (0, -2)):
            hail(along(rows, steps))
        for rows, cols in ((0, n_col // 2), (-1, 0), (-3, 0)):
            hail(at(rows, cols))

        @pl.when(hub)
        def _():
            hail(at(across - 2, 0))

        pl.semaphore_wait(barrier, 6 + jnp.where(hub | seam, 1, 0))

    flip = a_copy(a_flip, 3, 4, at(0, n_col // 2))
    flip.start()

    @pl.when(odd == 0)
    def _():
        @pl.when(lane + 1 < n_col // 2)
        def _():
            a_copy(a_one, 0, 0, along(0, 1)).start()

        listed = remote(
            tables.at[pl.ds(2, 2)], t_got.at[pl.ds(0, 2)], t_send.at[0], t_recv.at[0], at(-2, 0)
        )
        listed.start()
        mate = remote(b_hbm, b_mate, mate_send.at[0], mate_recv.at[0], at(1, 0))
        mate.start()
        own_tab = bring(tables, tab, 0)
        own_a = bring(a_hbm, a_own, 1)
        own_b = bring(b_hbm, b_own, 2)
        sums[NONE] = jnp.zeros((BS, BS), jnp.float32)
        own_tab.wait()
        own_a.wait()
        own_b.wait()
        products(a_own, b_own, tab, 0)
        collect(acc, tab, 0, False)
        flip.wait_recv()
        left = a_copy(a_one, 0, 0, along(0, 1))
        far = a_copy(a_even, 2, 2, along(-2, 3))
        two = a_copy(a_two, 1, 1, along(-2, 2))
        a_start(a_even, 2, 2, along(-2, 3), 3)

        listed.wait_recv()
        remote(
            tables.at[pl.ds(3, 1)], t_got.at[pl.ds(2, 1)], t_send.at[0], t_recv.at[1], at(1, 0)
        ).wait_recv()
        got = pltpu.make_async_copy(t_got, tab_next, smem_sem.at[0])
        got.start()
        got.wait()
        far.wait_send()
        a_start(a_two, 1, 1, along(-2, 2), 2)

        a_copy(a_odd, 2, 3, at(1, 0)).wait_recv()
        products(a_odd, b_own, tab_next, 2)

        def one(k, carry):
            encode_chunk(k, lambda c: sums[tab_next[2, 3, c]], code_one)
            return carry

        lax.fori_loop(0, NC, one, 0)

        def send_one(k, carry):
            remote(code_one.at[k], code_in.at[k], one_send.at[k], c_recv.at[k], at(3, 0)).start()
            return carry

        @pl.when(at_start)
        def _():
            lax.fori_loop(0, NC, send_one, 0)

        def pass_on(k, carry):
            copy = remote(
                b_chunk(b_prev, k), b_chunk(b_prev, k), b_send.at[k], b_recv.at[k], at(1, 0)
            )
            copy.wait_recv()
            copy.start()
            return carry

        lax.fori_loop(0, NB, pass_on, 0)

        @pl.when(jnp.logical_not(at_start))
        def _():
            lax.fori_loop(0, NC, send_one, 0)

        far.wait_recv()
        products(a_even, b_prev, tab_next, 1)
        collect(part, tab_next, 1, False)
        two.wait_recv()
        products(a_two, b_own, tab_next, 0)

        def zero(k, carry):
            encode_chunk(k, lambda c: part[c] + sums[tab_next[0, 3, c]], code_zero)
            remote(code_zero.at[k], code_in.at[k], zero_send.at[k], c_recv.at[k], at(2, 0)).start()
            return carry

        lax.fori_loop(0, NC, zero, 0)
        two.wait_send()

        @pl.when(lane + 1 >= n_col // 2)
        def _():
            a_copy(a_one, 0, 0, along(0, 1), a_flip).start()

        left.wait_recv()
        products(a_one, b_prev, tab, 1)
        collect(acc, tab, 1, True)
        left.wait_send()
        flip.wait_send()
        listed.wait_send()
        mate.wait_send()

        def drained(k, carry):
            remote(
                b_chunk(b_prev, k), b_chunk(b_prev, k), b_send.at[k], b_recv.at[k], at(1, 0)
            ).wait_send()
            return carry

        lax.fori_loop(0, NB, drained, 0)
        finish()

        def gone(k, carry):
            remote(code_one.at[k], code_in.at[k], one_send.at[k], c_recv.at[k], at(3, 0)).wait_send()
            remote(code_zero.at[k], code_in.at[k], zero_send.at[k], c_recv.at[k], at(2, 0)).wait_send()
            return carry

        lax.fori_loop(0, NC, gone, 0)

    @pl.when(odd == 1)
    def _():
        def b_copy(k):
            return remote(
                b_chunk(b_hbm, k), b_chunk(b_prev, k), b_send.at[k], b_recv.at[k], at(1, 0)
            )

        def to_hub(k):
            return remote(
                b_chunk(b_hbm, k),
                (a_even, a_odd)[k - 2],
                b_send.at[k],
                hub_recv.at[k - 2],
                at(2 - across, 0),
            )

        def from_hub(k):
            return remote(
                (a_even, a_odd)[k - 2],
                b_chunk(b_prev, k),
                hub_send.at[k - 2],
                b_recv.at[k],
                at(across - 1, 0),
            )

        @pl.when(seam)
        def _():
            for k in RELAYED:
                to_hub(k).start()

        @pl.when(jnp.logical_not(seam))
        def _():
            for k in range(NB):
                b_copy(k).start()

        listed = remote(
            tables.at[pl.ds(3, 1)], t_got.at[pl.ds(2, 1)], t_send.at[0], t_recv.at[1], at(-3, 0)
        )
        listed.start()
        own_tab = bring(tables, tab, 0)
        own_a = bring(a_hbm, a_own, 1)
        own_b = bring(b_hbm, b_own, 2)

        @pl.when(lane + 1 < n_col // 2)
        def _():
            a_copy(a_one, 0, 0, along(0, 1)).start()

        sums[NONE] = jnp.zeros((BS, BS), jnp.float32)
        own_tab.wait()
        own_a.wait()
        own_b.wait()
        products(a_own, b_own, tab, 0)
        collect(acc, tab, 0, False)
        flip.wait_recv()
        left = a_copy(a_one, 0, 0, along(0, 1))
        far = a_copy(a_odd, 2, 3, along(-3, 3))
        two = a_copy(a_two, 1, 1, along(0, 2))
        a_start(a_odd, 2, 3, along(-3, 3), 3)

        @pl.when(seam)
        def _():
            for k in DIRECT:
                b_copy(k).start()

        far.wait_send()

        @pl.when(lane + 1 >= n_col // 2)
        def _():
            a_copy(a_one, 0, 0, along(0, 1), a_flip).start()
        @pl.when(hub)
        def _():
            for k in RELAYED:
                to_hub(k).wait_recv()
                from_hub(k).start()

        def absorb_and_send(k, carry):
            absorb(k)

            @pl.when(k == 0)
            def _():
                a_start(a_two, 1, 1, along(0, 2), 2)

            return carry

        lax.fori_loop(0, NC, absorb_and_send, 0)
        remote(b_hbm, b_mate, mate_send.at[0], mate_recv.at[0], at(-1, 0)).wait_recv()
        left.wait_recv()
        products(a_one, b_mate, tab, 1)
        collect(acc, tab, 1, True)
        two.wait_recv()
        for k in range(NB):
            b_copy(k).wait_recv()
        products(a_two, b_prev, tab, 2)
        collect(acc, tab, 2, True)
        shown = pltpu.make_async_copy(acc, out, out_sem.at[0])
        shown.start()
        left.wait_send()
        two.wait_send()
        flip.wait_send()
        listed.wait_send()
        for k in range(NB):
            b_copy(k).wait_send()

        @pl.when(hub)
        def _():
            for k in RELAYED:
                from_hub(k).wait_send()

        shown.wait()


def grid_product(tables, a, b):
    anywhere = pl.BlockSpec(memory_space=pl.ANY)
    left = pltpu.VMEM((SA, BS, BS), jnp.bfloat16)
    right = pltpu.VMEM((SB, BS, BS), jnp.bfloat16)
    code = pltpu.VMEM((NC, CODED_ROWS, BS), jnp.int16)
    dma = pltpu.SemaphoreType.DMA
    return pl.pallas_call(
        kernel,
        out_shape=jax.ShapeDtypeStruct((CBLK, BS, BS), jnp.float32),
        in_specs=[anywhere] * 3,
        out_specs=anywhere,
        scratch_shapes=[left] * 6
        + [right] * 3
        + [
            pltpu.VMEM((3, 4, NP), jnp.int32),
            pltpu.SMEM((STEPS, 4, NP), jnp.int32),
            pltpu.SMEM((3, 4, NP), jnp.int32),
            pltpu.VMEM((NP + 1, BS, BS), jnp.float32),
            pltpu.VMEM((CBLK, BS, BS), jnp.float32),
            pltpu.VMEM((CBLK, BS, BS), jnp.float32),
        ]
        + [code] * 3
        + [
            dma((5,)),
            dma((4,)),
            dma((2,)),
            dma((1,)),
            dma((1,)),
            dma((1,)),
            dma((NB,)),
            dma((NB,)),
            dma((2,)),
            dma((2,)),
            dma((NC,)),
            dma((NC,)),
            dma((NC,)),
            dma((3,)),
            dma((1,)),
            dma((NC,)),
        ],
        compiler_params=pltpu.CompilerParams(
            collective_id=0, has_side_effects=True, vmem_limit_bytes=58 << 20
        ),
        cost_estimate=pl.CostEstimate(
            flops=2 * STEPS * NP * BS**3, bytes_accessed=32 << 20, transcendentals=0
        ),
    )(tables, a, b)


def listed(pairs):
    target = pairs[:, 2, :]
    slot = jnp.arange(NP, dtype=jnp.int32)
    same = (target[:, :, None] == target[:, None, :]) & (slot[:, None] < slot[None, :])
    before = jnp.max(jnp.where(same, slot[:, None], -1), axis=1)
    hit = target[:, :, None] == slot[None, None, :]
    final = jnp.max(jnp.where(hit, slot[:, None], -1), axis=1)
    found = jnp.stack([before, final], axis=1)
    found = jnp.where(found < 0, NONE, found)
    return jnp.concatenate([pairs[:, :2, :], found], axis=1)


def on_device(a_blocks, b_blocks, pairs):
    return grid_product(listed(pairs[0, 0]), a_blocks[0, 0], b_blocks[0, 0])[None, None]


def solution(mesh):
    spec = P("row", "col", None, None, None)
    return jax.shard_map(
        on_device, mesh=mesh, in_specs=(spec,) * 3, out_specs=spec, check_vma=False
    )
```

```python
import jax
import jax.numpy as jnp
from jax import lax
from jax.experimental import pallas as pl
from jax.experimental.pallas import tpu as pltpu
from jax.sharding import PartitionSpec as P

BS = 128
SA = 32
SB = 128
NP = 256
CBLK = 64
STEPS = 4
UNROLL = 16
NC = 4
PER = CBLK // NC
CODED_ROWS = PER * BS + PER
NB = 4
BPER = SB // NB
RELAYED = (3,)
DIRECT = tuple(k for k in range(NB) if k not in RELAYED)
NONE = NP
MESH = pl.DeviceIdType.MESH


def encode(value):
    top = jnp.max(jnp.abs(value), axis=0, keepdims=True)
    exponent = jnp.ceil(jnp.log2(jnp.maximum(top, 1e-30)) + 2e-4) - 15.0
    coded = jnp.round(value * jnp.exp2(-exponent)).astype(jnp.int32).astype(jnp.int16)
    return coded, exponent


def kernel(
    tables,
    a_hbm,
    b_hbm,
    acc,
    a_one,
    a_two,
    a_even,
    a_odd,
    a_own,
    a_flip,
    b_own,
    b_prev,
    b_mate,
    t_got,
    tab,
    tab_next,
    sums,
    part,
    code_one,
    code_zero,
    code_in,
    a_recv,
    a_send,
    t_recv,
    t_send,
    mate_recv,
    mate_send,
    b_recv,
    b_send,
    hub_recv,
    hub_send,
    c_recv,
    zero_send,
    one_send,
    local,
    smem_sem,
):
    n_row, n_col = lax.axis_size("row"), lax.axis_size("col")
    row, col = lax.axis_index("row"), lax.axis_index("col")
    odd = lax.rem(row, 2)

    def at(rows, cols):
        return (lax.rem(row + rows + n_row, n_row), lax.rem(col + cols + n_col, n_col))

    def remote(src, dst, send, recv, to):
        return pltpu.make_async_remote_copy(
            src_ref=src, dst_ref=dst, send_sem=send, recv_sem=recv, device_id=to, device_id_type=MESH
        )

    def products(a, b, tab_ref, j):
        def group(g, carry):
            for u in range(UNROLL):
                n = g * UNROLL + u
                product = jnp.dot(
                    a[tab_ref[j, 0, n]], b[tab_ref[j, 1, n]], preferred_element_type=jnp.float32
                )
                sums[n] = sums[tab_ref[j, 2, n]] + product
            return carry

        lax.fori_loop(0, NP // UNROLL, group, 0)

    def collect(dst, tab_ref, j, add):
        def some(g, carry):
            for u in range(8):
                c = g * 8 + u
                value = sums[tab_ref[j, 3, c]]
                dst[c] = dst[c] + value if add else value
            return carry

        lax.fori_loop(0, CBLK // 8, some, 0)

    def encode_chunk(k, block_of, code):
        exponents = []
        for u in range(PER):
            coded, exponent = encode(block_of(k * PER + u))
            code[k, pl.ds(u * BS, BS), :] = coded
            exponents.append(exponent)
        rows = jnp.concatenate(exponents, axis=0).astype(jnp.int32).astype(jnp.int16)
        code[k, pl.ds(PER * BS, PER), :] = rows

    lane = lax.rem(col, n_col // 2)
    plane = col - lane

    def along(rows, steps):
        half = n_col // 2
        return (lax.rem(row + rows + n_row, n_row), plane + lax.rem(lane + steps + half, half))

    def a_copy(dst, slot, index, to, src=None):
        return remote(a_hbm if src is None else src, dst, a_send.at[slot], a_recv.at[index], to)

    def a_start(dst, slot, index, to, steps):
        @pl.when(lane + steps < n_col // 2)
        def _():
            a_copy(dst, slot, index, to).start()

        @pl.when(lane + steps >= n_col // 2)
        def _():
            a_copy(dst, slot, index, to, a_flip).start()

    def b_chunk(ref, k):
        return ref.at[pl.ds(k * BPER, BPER)]

    def bring(src, dst, k):
        copy = pltpu.make_async_copy(src, dst, local.at[k])
        copy.start()
        return copy

    def absorb(k):
        remote(code_in.at[k], code_in.at[k], zero_send.at[k], c_recv.at[k], at(1, 0)).wait_recv()
        rows = code_in[k, pl.ds(PER * BS, PER), :].astype(jnp.int32).astype(jnp.float32)
        for u in range(PER):
            c = k * PER + u
            coded = code_in[k, pl.ds(u * BS, BS), :].astype(jnp.int32).astype(jnp.float32)
            acc[c] = acc[c] + coded * jnp.exp2(rows[u : u + 1])

    def finish():
        def chunk(k, carry):
            absorb(k)
            return carry

        lax.fori_loop(0, NC, chunk, 0)

    barrier = pltpu.get_barrier_semaphore()
    place = lax.rem(row, n_row // 2)
    at_start = place == 0
    hub = place == 1
    seam = place == n_row // 2 - 1
    across = n_row // 2

    def hail(to):
        pl.semaphore_signal(barrier, inc=1, device_id=to, device_id_type=MESH)

    @pl.when(odd == 0)
    def _():
        for rows, steps in ((0, -1), (2, -2), (2, -3), (3, -3)):
            hail(along(rows, steps))
        for rows, cols in ((0, n_col // 2), (2, 0), (3, 0), (-1, 0), (-2, 0)):
            hail(at(rows, cols))

        @pl.when(at_start)
        def _():
            hail(at(across + 1, 0))

        pl.semaphore_wait(barrier, 8)

    @pl.when(odd == 1)
    def _():
        for rows, steps in ((0, -1), (0, -2)):
            hail(along(rows, steps))
        for rows, cols in ((0, n_col // 2), (-1, 0), (-3, 0)):
            hail(at(rows, cols))

        @pl.when(hub)
        def _():
            hail(at(across - 2, 0))

        pl.semaphore_wait(barrier, 6 + jnp.where(hub | seam, 1, 0))

    flip = a_copy(a_flip, 3, 4, at(0, n_col // 2))
    flip.start()

    @pl.when(odd == 0)
    def _():
        @pl.when(lane + 1 < n_col // 2)
        def _():
            a_copy(a_one, 0, 0, along(0, 1)).start()

        listed = remote(
            tables.at[pl.ds(2, 2)], t_got.at[pl.ds(0, 2)], t_send.at[0], t_recv.at[0], at(-2, 0)
        )
        listed.start()
        mate = remote(b_hbm, b_mate, mate_send.at[0], mate_recv.at[0], at(1, 0))
        mate.start()
        own_tab = bring(tables, tab, 0)
        own_a = bring(a_hbm, a_own, 1)
        own_b = bring(b_hbm, b_own, 2)
        sums[NONE] = jnp.zeros((BS, BS), jnp.float32)
        own_tab.wait()
        own_a.wait()
        own_b.wait()
        products(a_own, b_own, tab, 0)
        collect(acc, tab, 0, False)
        flip.wait_recv()
        left = a_copy(a_one, 0, 0, along(0, 1))
        far = a_copy(a_even, 2, 2, along(-2, 3))
        two = a_copy(a_two, 1, 1, along(-2, 2))
        a_start(a_even, 2, 2, along(-2, 3), 3)

        listed.wait_recv()
        remote(
            tables.at[pl.ds(3, 1)], t_got.at[pl.ds(2, 1)], t_send.at[0], t_recv.at[1], at(1, 0)
        ).wait_recv()
        got = pltpu.make_async_copy(t_got, tab_next, smem_sem.at[0])
        got.start()
        got.wait()
        far.wait_send()
        a_start(a_two, 1, 1, along(-2, 2), 2)

        a_copy(a_odd, 2, 3, at(1, 0)).wait_recv()
        products(a_odd, b_own, tab_next, 2)

        def one(k, carry):
            encode_chunk(k, lambda c: sums[tab_next[2, 3, c]], code_one)
            return carry

        lax.fori_loop(0, NC, one, 0)

        def send_one(k, carry):
            remote(code_one.at[k], code_in.at[k], one_send.at[k], c_recv.at[k], at(3, 0)).start()
            return carry

        @pl.when(at_start)
        def _():
            lax.fori_loop(0, NC, send_one, 0)

        def pass_on(k, carry):
            copy = remote(
                b_chunk(b_prev, k), b_chunk(b_prev, k), b_send.at[k], b_recv.at[k], at(1, 0)
            )
            copy.wait_recv()
            copy.start()
            return carry

        lax.fori_loop(0, NB, pass_on, 0)

        @pl.when(jnp.logical_not(at_start))
        def _():
            lax.fori_loop(0, NC, send_one, 0)

        far.wait_recv()
        products(a_even, b_prev, tab_next, 1)
        collect(part, tab_next, 1, False)
        two.wait_recv()
        products(a_two, b_own, tab_next, 0)

        def zero(k, carry):
            encode_chunk(k, lambda c: part[c] + sums[tab_next[0, 3, c]], code_zero)
            remote(code_zero.at[k], code_in.at[k], zero_send.at[k], c_recv.at[k], at(2, 0)).start()
            return carry

        lax.fori_loop(0, NC, zero, 0)
        two.wait_send()

        @pl.when(lane + 1 >= n_col // 2)
        def _():
            a_copy(a_one, 0, 0, along(0, 1), a_flip).start()

        left.wait_recv()
        products(a_one, b_prev, tab, 1)
        collect(acc, tab, 1, True)
        left.wait_send()
        flip.wait_send()
        listed.wait_send()
        mate.wait_send()

        def drained(k, carry):
            remote(
                b_chunk(b_prev, k), b_chunk(b_prev, k), b_send.at[k], b_recv.at[k], at(1, 0)
            ).wait_send()
            return carry

        lax.fori_loop(0, NB, drained, 0)
        finish()

        def gone(k, carry):
            remote(code_one.at[k], code_in.at[k], one_send.at[k], c_recv.at[k], at(3, 0)).wait_send()
            remote(code_zero.at[k], code_in.at[k], zero_send.at[k], c_recv.at[k], at(2, 0)).wait_send()
            return carry

        lax.fori_loop(0, NC, gone, 0)

    @pl.when(odd == 1)
    def _():
        def b_copy(k):
            return remote(
                b_chunk(b_hbm, k), b_chunk(b_prev, k), b_send.at[k], b_recv.at[k], at(1, 0)
            )

        def to_hub(k):
            return remote(
                b_chunk(b_hbm, k),
                (a_even, a_odd)[k - 2],
                b_send.at[k],
                hub_recv.at[k - 2],
                at(2 - across, 0),
            )

        def from_hub(k):
            return remote(
                (a_even, a_odd)[k - 2],
                b_chunk(b_prev, k),
                hub_send.at[k - 2],
                b_recv.at[k],
                at(across - 1, 0),
            )

        @pl.when(seam)
        def _():
            for k in RELAYED:
                to_hub(k).start()

        @pl.when(jnp.logical_not(seam))
        def _():
            for k in range(NB):
                b_copy(k).start()

        listed = remote(
            tables.at[pl.ds(3, 1)], t_got.at[pl.ds(2, 1)], t_send.at[0], t_recv.at[1], at(-3, 0)
        )
        listed.start()
        own_tab = bring(tables, tab, 0)
        own_a = bring(a_hbm, a_own, 1)
        own_b = bring(b_hbm, b_own, 2)

        @pl.when(lane + 1 < n_col // 2)
        def _():
            a_copy(a_one, 0, 0, along(0, 1)).start()

        sums[NONE] = jnp.zeros((BS, BS), jnp.float32)
        own_tab.wait()
        own_a.wait()
        own_b.wait()
        products(a_own, b_own, tab, 0)
        collect(acc, tab, 0, False)
        flip.wait_recv()
        left = a_copy(a_one, 0, 0, along(0, 1))
        far = a_copy(a_odd, 2, 3, along(-3, 3))
        two = a_copy(a_two, 1, 1, along(0, 2))
        a_start(a_odd, 2, 3, along(-3, 3), 3)

        @pl.when(seam)
        def _():
            for k in DIRECT:
                b_copy(k).start()

        far.wait_send()

        @pl.when(lane + 1 >= n_col // 2)
        def _():
            a_copy(a_one, 0, 0, along(0, 1), a_flip).start()
        @pl.when(hub)
        def _():
            for k in RELAYED:
                to_hub(k).wait_recv()
                from_hub(k).start()

        def absorb_and_send(k, carry):
            absorb(k)

            @pl.when(k == 0)
            def _():
                a_start(a_two, 1, 1, along(0, 2), 2)

            return carry

        lax.fori_loop(0, NC, absorb_and_send, 0)
        remote(b_hbm, b_mate, mate_send.at[0], mate_recv.at[0], at(-1, 0)).wait_recv()
        left.wait_recv()
        products(a_one, b_mate, tab, 1)
        collect(acc, tab, 1, True)
        two.wait_recv()
        for k in range(NB):
            b_copy(k).wait_recv()
        products(a_two, b_prev, tab, 2)
        collect(acc, tab, 2, True)
        left.wait_send()
        two.wait_send()
        flip.wait_send()
        listed.wait_send()
        for k in range(NB):
            b_copy(k).wait_send()

        @pl.when(hub)
        def _():
            for k in RELAYED:
                from_hub(k).wait_send()


def grid_product(tables, a, b):
    anywhere = pl.BlockSpec(memory_space=pl.ANY)
    in_hbm = pl.BlockSpec(memory_space=pltpu.HBM)
    left = pltpu.VMEM((SA, BS, BS), jnp.bfloat16)
    right = pltpu.VMEM((SB, BS, BS), jnp.bfloat16)
    code = pltpu.VMEM((NC, CODED_ROWS, BS), jnp.int16)
    dma = pltpu.SemaphoreType.DMA
    return pl.pallas_call(
        kernel,
        out_shape=jax.ShapeDtypeStruct((CBLK, BS, BS), jnp.float32),
        in_specs=[anywhere, in_hbm, in_hbm],
        out_specs=pl.BlockSpec(memory_space=pltpu.VMEM),
        scratch_shapes=[left] * 6
        + [right] * 3
        + [
            pltpu.VMEM((3, 4, NP), jnp.int32),
            pltpu.SMEM((STEPS, 4, NP), jnp.int32),
            pltpu.SMEM((3, 4, NP), jnp.int32),
            pltpu.VMEM((NP + 1, BS, BS), jnp.float32),
            pltpu.VMEM((CBLK, BS, BS), jnp.float32),
        ]
        + [code] * 3
        + [
            dma((5,)),
            dma((4,)),
            dma((2,)),
            dma((1,)),
            dma((1,)),
            dma((1,)),
            dma((NB,)),
            dma((NB,)),
            dma((2,)),
            dma((2,)),
            dma((NC,)),
            dma((NC,)),
            dma((NC,)),
            dma((3,)),
            dma((1,)),
        ],
        compiler_params=pltpu.CompilerParams(
            collective_id=0, has_side_effects=True, vmem_limit_bytes=48 << 20
        ),
        cost_estimate=pl.CostEstimate(
            flops=2 * STEPS * NP * BS**3, bytes_accessed=32 << 20, transcendentals=0
        ),
    )(tables, a, b)


def listed(pairs):
    target = pairs[:, 2, :]
    slot = jnp.arange(NP, dtype=jnp.int32)
    same = (target[:, :, None] == target[:, None, :]) & (slot[:, None] < slot[None, :])
    before = jnp.max(jnp.where(same, slot[:, None], -1), axis=1)
    hit = target[:, :, None] == slot[None, None, :]
    final = jnp.max(jnp.where(hit, slot[:, None], -1), axis=1)
    found = jnp.stack([before, final], axis=1)
    found = jnp.where(found < 0, NONE, found)
    return jnp.concatenate([pairs[:, :2, :], found], axis=1)


def on_device(a_blocks, b_blocks, pairs):
    return grid_product(listed(pairs[0, 0]), a_blocks[0, 0], b_blocks[0, 0])[None, None]


def solution(mesh):
    spec = P("row", "col", None, None, None)
    return jax.shard_map(
        on_device, mesh=mesh, in_specs=(spec,) * 3, out_specs=spec, check_vma=False
    )
```

```python
import jax
import jax.numpy as jnp
from jax import lax
from jax.experimental import pallas as pl
from jax.experimental.pallas import tpu as pltpu
from jax.sharding import PartitionSpec as P

BS = 128
SA = 32
SB = 128
NP = 256
CBLK = 64
STEPS = 4
UNROLL = 16
NC = 4
PER = CBLK // NC
CODED_ROWS = PER * BS + PER
NB = 4
BPER = SB // NB
RELAYED = (3,)
DIRECT = tuple(k for k in range(NB) if k not in RELAYED)
NONE = NP
MESH = pl.DeviceIdType.MESH


def encode(value):
    top = jnp.max(jnp.abs(value), axis=0, keepdims=True)
    exponent = jnp.ceil(jnp.log2(jnp.maximum(top, 1e-30)) + 2e-4) - 15.0
    coded = jnp.round(value * jnp.exp2(-exponent)).astype(jnp.int32).astype(jnp.int16)
    return coded, exponent


def kernel(
    tables,
    a_hbm,
    b_hbm,
    acc,
    a_one,
    a_two,
    a_even,
    a_odd,
    a_own,
    a_flip,
    b_own,
    b_prev,
    b_mate,
    t_got,
    tab,
    tab_next,
    sums,
    part,
    code_one,
    code_zero,
    code_in,
    a_recv,
    a_send,
    t_recv,
    t_send,
    mate_recv,
    mate_send,
    b_recv,
    b_send,
    hub_recv,
    hub_send,
    c_recv,
    zero_send,
    one_send,
    local,
    smem_sem,
):
    n_row, n_col = lax.axis_size("row"), lax.axis_size("col")
    row, col = lax.axis_index("row"), lax.axis_index("col")
    odd = lax.rem(row, 2)

    def at(rows, cols):
        return (lax.rem(row + rows + n_row, n_row), lax.rem(col + cols + n_col, n_col))

    def remote(src, dst, send, recv, to):
        return pltpu.make_async_remote_copy(
            src_ref=src, dst_ref=dst, send_sem=send, recv_sem=recv, device_id=to, device_id_type=MESH
        )

    def products(a, b, tab_ref, j):
        def group(g, carry):
            for u in range(UNROLL):
                n = g * UNROLL + u
                product = jnp.dot(
                    a[tab_ref[j, 0, n]], b[tab_ref[j, 1, n]], preferred_element_type=jnp.float32
                )
                sums[n] = sums[tab_ref[j, 2, n]] + product
            return carry

        lax.fori_loop(0, NP // UNROLL, group, 0)

    def collect(dst, tab_ref, j, add):
        def some(g, carry):
            for u in range(8):
                c = g * 8 + u
                value = sums[tab_ref[j, 3, c]]
                dst[c] = dst[c] + value if add else value
            return carry

        lax.fori_loop(0, CBLK // 8, some, 0)

    def encode_chunk(k, block_of, code):
        exponents = []
        for u in range(PER):
            coded, exponent = encode(block_of(k * PER + u))
            code[k, pl.ds(u * BS, BS), :] = coded
            exponents.append(exponent)
        rows = jnp.concatenate(exponents, axis=0).astype(jnp.int32).astype(jnp.int16)
        code[k, pl.ds(PER * BS, PER), :] = rows

    lane = lax.rem(col, n_col // 2)
    plane = col - lane

    def along(rows, steps):
        half = n_col // 2
        return (lax.rem(row + rows + n_row, n_row), plane + lax.rem(lane + steps + half, half))

    def a_copy(dst, slot, index, to, src=None):
        return remote(a_hbm if src is None else src, dst, a_send.at[slot], a_recv.at[index], to)

    def a_start(dst, slot, index, to, steps):
        @pl.when(lane + steps < n_col // 2)
        def _():
            a_copy(dst, slot, index, to).start()

        @pl.when(lane + steps >= n_col // 2)
        def _():
            a_copy(dst, slot, index, to, a_flip).start()

    def b_chunk(ref, k):
        return ref.at[pl.ds(k * BPER, BPER)]

    def bring(src, dst, k):
        copy = pltpu.make_async_copy(src, dst, local.at[k])
        copy.start()
        return copy

    def absorb(k):
        remote(code_in.at[k], code_in.at[k], zero_send.at[k], c_recv.at[k], at(1, 0)).wait_recv()
        rows = code_in[k, pl.ds(PER * BS, PER), :].astype(jnp.int32).astype(jnp.float32)
        for u in range(PER):
            c = k * PER + u
            coded = code_in[k, pl.ds(u * BS, BS), :].astype(jnp.int32).astype(jnp.float32)
            acc[c] = acc[c] + coded * jnp.exp2(rows[u : u + 1])

    def finish():
        def chunk(k, carry):
            absorb(k)
            return carry

        lax.fori_loop(0, NC, chunk, 0)

    barrier = pltpu.get_barrier_semaphore()
    place = lax.rem(row, n_row // 2)
    at_start = place == 0
    hub = place == 1
    seam = place == n_row // 2 - 1
    across = n_row // 2

    def hail(to):
        pl.semaphore_signal(barrier, inc=1, device_id=to, device_id_type=MESH)

    @pl.when(odd == 0)
    def _():
        for rows, steps in ((0, -1), (2, -2), (2, -3), (3, -3)):
            hail(along(rows, steps))
        for rows, cols in ((0, n_col // 2), (2, 0), (3, 0), (-1, 0), (-2, 0)):
            hail(at(rows, cols))

        @pl.when(at_start)
        def _():
            hail(at(across + 1, 0))

        pl.semaphore_wait(barrier, 8)

    @pl.when(odd == 1)
    def _():
        for rows, steps in ((0, -1), (0, -2)):
            hail(along(rows, steps))
        for rows, cols in ((0, n_col // 2), (-1, 0), (-3, 0)):
            hail(at(rows, cols))

        @pl.when(hub)
        def _():
            hail(at(across - 2, 0))

        pl.semaphore_wait(barrier, 6 + jnp.where(hub | seam, 1, 0))

    flip = a_copy(a_flip, 3, 4, at(0, n_col // 2))
    flip.start()

    @pl.when(odd == 0)
    def _():
        @pl.when(lane + 1 < n_col // 2)
        def _():
            a_copy(a_one, 0, 0, along(0, 1)).start()

        listed = remote(
            tables.at[pl.ds(2, 2)], t_got.at[pl.ds(0, 2)], t_send.at[0], t_recv.at[0], at(-2, 0)
        )
        listed.start()
        mate = remote(b_hbm, b_mate, mate_send.at[0], mate_recv.at[0], at(1, 0))
        mate.start()
        own_tab = bring(tables, tab, 0)
        own_a = bring(a_hbm, a_own, 1)
        own_b = bring(b_hbm, b_own, 2)
        sums[NONE] = jnp.zeros((BS, BS), jnp.float32)
        own_tab.wait()
        own_a.wait()
        own_b.wait()
        products(a_own, b_own, tab, 0)
        collect(acc, tab, 0, False)
        flip.wait_recv()
        left = a_copy(a_one, 0, 0, along(0, 1))
        far = a_copy(a_even, 2, 2, along(-2, 3))
        two = a_copy(a_two, 1, 1, along(-2, 2))
        a_start(a_even, 2, 2, along(-2, 3), 3)

        listed.wait_recv()
        remote(
            tables.at[pl.ds(3, 1)], t_got.at[pl.ds(2, 1)], t_send.at[0], t_recv.at[1], at(1, 0)
        ).wait_recv()
        got = pltpu.make_async_copy(t_got, tab_next, smem_sem.at[0])
        got.start()
        got.wait()
        far.wait_send()
        a_start(a_two, 1, 1, along(-2, 2), 2)

        a_copy(a_odd, 2, 3, at(1, 0)).wait_recv()
        products(a_odd, b_own, tab_next, 2)

        def one(k, carry):
            encode_chunk(k, lambda c: sums[tab_next[2, 3, c]], code_one)
            return carry

        lax.fori_loop(0, NC, one, 0)

        def send_one(k, carry):
            remote(code_one.at[k], code_in.at[k], one_send.at[k], c_recv.at[k], at(3, 0)).start()
            return carry

        @pl.when(at_start)
        def _():
            lax.fori_loop(0, NC, send_one, 0)

        @pl.when(at_start)
        def _():
            two.wait_recv()
            products(a_two, b_own, tab_next, 0)
            collect(part, tab_next, 0, False)

        def pass_on(k, carry):
            copy = remote(
                b_chunk(b_prev, k), b_chunk(b_prev, k), b_send.at[k], b_recv.at[k], at(1, 0)
            )
            copy.wait_recv()
            copy.start()
            return carry

        lax.fori_loop(0, NB, pass_on, 0)

        @pl.when(jnp.logical_not(at_start))
        def _():
            lax.fori_loop(0, NC, send_one, 0)

        far.wait_recv()
        products(a_even, b_prev, tab_next, 1)

        @pl.when(jnp.logical_not(at_start))
        def _():
            collect(part, tab_next, 1, False)
            two.wait_recv()
            products(a_two, b_own, tab_next, 0)

        own_step = jnp.where(at_start, 1, 0)

        def zero(k, carry):
            encode_chunk(k, lambda c: part[c] + sums[tab_next[own_step, 3, c]], code_zero)
            remote(code_zero.at[k], code_in.at[k], zero_send.at[k], c_recv.at[k], at(2, 0)).start()
            return carry

        lax.fori_loop(0, NC, zero, 0)
        two.wait_send()

        @pl.when(lane + 1 >= n_col // 2)
        def _():
            a_copy(a_one, 0, 0, along(0, 1), a_flip).start()

        left.wait_recv()
        products(a_one, b_prev, tab, 1)
        collect(acc, tab, 1, True)
        left.wait_send()
        flip.wait_send()
        listed.wait_send()
        mate.wait_send()

        def drained(k, carry):
            remote(
                b_chunk(b_prev, k), b_chunk(b_prev, k), b_send.at[k], b_recv.at[k], at(1, 0)
            ).wait_send()
            return carry

        lax.fori_loop(0, NB, drained, 0)
        finish()

        def gone(k, carry):
            remote(code_one.at[k], code_in.at[k], one_send.at[k], c_recv.at[k], at(3, 0)).wait_send()
            remote(code_zero.at[k], code_in.at[k], zero_send.at[k], c_recv.at[k], at(2, 0)).wait_send()
            return carry

        lax.fori_loop(0, NC, gone, 0)

    @pl.when(odd == 1)
    def _():
        def b_copy(k):
            return remote(
                b_chunk(b_hbm, k), b_chunk(b_prev, k), b_send.at[k], b_recv.at[k], at(1, 0)
            )

        def to_hub(k):
            return remote(
                b_chunk(b_hbm, k),
                (a_even, a_odd)[k - 2],
                b_send.at[k],
                hub_recv.at[k - 2],
                at(2 - across, 0),
            )

        def from_hub(k):
            return remote(
                (a_even, a_odd)[k - 2],
                b_chunk(b_prev, k),
                hub_send.at[k - 2],
                b_recv.at[k],
                at(across - 1, 0),
            )

        @pl.when(seam)
        def _():
            for k in RELAYED:
                to_hub(k).start()

        @pl.when(jnp.logical_not(seam))
        def _():
            for k in range(NB):
                b_copy(k).start()

        listed = remote(
            tables.at[pl.ds(3, 1)], t_got.at[pl.ds(2, 1)], t_send.at[0], t_recv.at[1], at(-3, 0)
        )
        listed.start()
        own_tab = bring(tables, tab, 0)
        own_a = bring(a_hbm, a_own, 1)
        own_b = bring(b_hbm, b_own, 2)

        @pl.when(lane + 1 < n_col // 2)
        def _():
            a_copy(a_one, 0, 0, along(0, 1)).start()

        sums[NONE] = jnp.zeros((BS, BS), jnp.float32)
        own_tab.wait()
        own_a.wait()
        own_b.wait()
        products(a_own, b_own, tab, 0)
        collect(acc, tab, 0, False)
        flip.wait_recv()
        left = a_copy(a_one, 0, 0, along(0, 1))
        far = a_copy(a_odd, 2, 3, along(-3, 3))
        two = a_copy(a_two, 1, 1, along(0, 2))
        a_start(a_odd, 2, 3, along(-3, 3), 3)

        @pl.when(seam)
        def _():
            for k in DIRECT:
                b_copy(k).start()

        far.wait_send()

        @pl.when(lane + 1 >= n_col // 2)
        def _():
            a_copy(a_one, 0, 0, along(0, 1), a_flip).start()
        @pl.when(hub)
        def _():
            for k in RELAYED:
                to_hub(k).wait_recv()
                from_hub(k).start()

        def absorb_and_send(k, carry):
            absorb(k)

            @pl.when(k == 0)
            def _():
                a_start(a_two, 1, 1, along(0, 2), 2)

            return carry

        lax.fori_loop(0, NC, absorb_and_send, 0)
        remote(b_hbm, b_mate, mate_send.at[0], mate_recv.at[0], at(-1, 0)).wait_recv()
        left.wait_recv()
        products(a_one, b_mate, tab, 1)
        collect(acc, tab, 1, True)
        two.wait_recv()
        for k in range(NB):
            b_copy(k).wait_recv()
        products(a_two, b_prev, tab, 2)
        collect(acc, tab, 2, True)
        left.wait_send()
        two.wait_send()
        flip.wait_send()
        listed.wait_send()
        for k in range(NB):
            b_copy(k).wait_send()

        @pl.when(hub)
        def _():
            for k in RELAYED:
                from_hub(k).wait_send()


def grid_product(tables, a, b):
    anywhere = pl.BlockSpec(memory_space=pl.ANY)
    in_hbm = pl.BlockSpec(memory_space=pltpu.HBM)
    left = pltpu.VMEM((SA, BS, BS), jnp.bfloat16)
    right = pltpu.VMEM((SB, BS, BS), jnp.bfloat16)
    code = pltpu.VMEM((NC, CODED_ROWS, BS), jnp.int16)
    dma = pltpu.SemaphoreType.DMA
    return pl.pallas_call(
        kernel,
        out_shape=jax.ShapeDtypeStruct((CBLK, BS, BS), jnp.float32),
        in_specs=[anywhere, in_hbm, in_hbm],
        out_specs=pl.BlockSpec(memory_space=pltpu.VMEM),
        scratch_shapes=[left] * 6
        + [right] * 3
        + [
            pltpu.VMEM((3, 4, NP), jnp.int32),
            pltpu.SMEM((STEPS, 4, NP), jnp.int32),
            pltpu.SMEM((3, 4, NP), jnp.int32),
            pltpu.VMEM((NP + 1, BS, BS), jnp.float32),
            pltpu.VMEM((CBLK, BS, BS), jnp.float32),
        ]
        + [code] * 3
        + [
            dma((5,)),
            dma((4,)),
            dma((2,)),
            dma((1,)),
            dma((1,)),
            dma((1,)),
            dma((NB,)),
            dma((NB,)),
            dma((2,)),
            dma((2,)),
            dma((NC,)),
            dma((NC,)),
            dma((NC,)),
            dma((3,)),
            dma((1,)),
        ],
        compiler_params=pltpu.CompilerParams(
            collective_id=0, has_side_effects=True, vmem_limit_bytes=48 << 20
        ),
        cost_estimate=pl.CostEstimate(
            flops=2 * STEPS * NP * BS**3, bytes_accessed=32 << 20, transcendentals=0
        ),
    )(tables, pltpu.with_memory_space_constraint(a, pltpu.HBM), b)


def listed(pairs):
    target = pairs[:, 2, :]
    slot = jnp.arange(NP, dtype=jnp.int32)
    same = (target[:, :, None] == target[:, None, :]) & (slot[:, None] < slot[None, :])
    before = jnp.max(jnp.where(same, slot[:, None], -1), axis=1)
    hit = target[:, :, None] == slot[None, None, :]
    final = jnp.max(jnp.where(hit, slot[:, None], -1), axis=1)
    found = jnp.stack([before, final], axis=1)
    found = jnp.where(found < 0, NONE, found)
    return jnp.concatenate([pairs[:, :2, :], found], axis=1)


def on_device(a_blocks, b_blocks, pairs):
    return grid_product(listed(pairs[0, 0]), a_blocks[0, 0], b_blocks[0, 0])[None, None]


def solution(mesh):
    spec = P("row", "col", None, None, None)
    return jax.shard_map(
        on_device, mesh=mesh, in_specs=(spec,) * 3, out_specs=spec, check_vma=False
    )
```
